32 devices in a mesh: seq: 16 (over z, y, core), chan: 2 (over x).
Axes of the slice: x: 2, y: 2, z: 4, core: 2. Of those that a mesh axis runs over, the one named last changes fastest.
Arguments:
- inputs: bfloat16 [512, 512, 512], P('chan', 'seq'), may hold values from -6 to 6
- gate_in: bfloat16 [512, 512, 512], P('chan', 'seq'), may hold values from -6 to 6
- gate_out: bfloat16 [512, 512, 512], P('seq', 'chan'), may hold values from -6 to 6
- cotangent: bfloat16 [512, 512, 512], P('seq', 'chan'), may hold values from -6 to 6
- mix_one: bfloat16 [512, 512, 512], P('seq', 'chan'), may hold values from -6 to 6
- second_mixing_blocks: bfloat16 [512, 512, 512], P('seq', 'chan'), may hold values from -6 to 6
Outputs:
- grad_input: bfloat16 [512, 512, 512], P('chan', 'seq')
- grad_gate_out: bfloat16 [512, 512, 512], P('seq', 'chan')
- grad_mix_one: bfloat16 [512, 512, 512], P('seq', 'chan')
- grad_mix_two: bfloat16 [512, 512, 512], P('seq', 'chan')
The draws below stay inside these ranges and needn't reach their ends.
All inputs are finite; a program needn't handle non-finite values.
Results may differ from the reference program's by a relative error of at most 0.0095.
Values may be sent and summed in bfloat16 or wider, within the bound.
A program may use at most 256 MiB of HBM per device.

```python
import math
import jax
import jax.numpy as jnp
from jax import lax

D = 512
R = 512
C = 512
N_CHAN = 2


def level_of(own_key, shape, shards, low, high):
    level, own = 1.0, jax.random.fold_in(own_key, 6)
    for dim, shards_of in shards:
        steps = jnp.exp(jax.random.uniform(jax.random.fold_in(own, dim), (shards_of,), jnp.float32, low / len(shards), high / len(shards)))
        level = level * jnp.repeat(steps, shape[dim] // shards_of).reshape([-1 if axis == dim else 1 for axis in range(len(shape))])
    return level


def scatter_about(rng, extent, scale, most, split=(), dtype=jnp.bfloat16):
    level = level_of(rng, extent, split, -0.22, 0.18) if split else 1.0
    drawn = jax.random.normal(rng, extent, jnp.float32) * scale * level
    return jnp.minimum(jnp.maximum(drawn, -most), most).astype(dtype)


def setup_inputs(seed: int = 0) -> dict:
    key_of = jax.random.split(jax.random.key(seed), 7)
    return {
        "inputs": scatter_about(key_of[0], (D, R, C), 1.0, 6.0, ((0, 2), (1, 16))),
        "gate_in": scatter_about(key_of[1], (D, R, C), 1.0, 6.0, ((0, 2), (1, 16))),
        "gate_out": scatter_about(key_of[2], (C, D, R), 1.0, 6.0, ((0, 16), (1, 2))),
        "cotangent": scatter_about(key_of[3], (C, D, R), 1.0, 6.0, ((0, 16), (1, 2))),
        "mix_one": scatter_about(key_of[4], (R, C, C), 1.0, 6.0, ((0, 16), (1, 2))),
        "second_mixing_blocks": scatter_about(key_of[5], (C, R, R), 1.0, 6.0, ((0, 16), (1, 2))),
    }


def reference(inputs, gate_in, gate_out, cotangent, mix_one, second_mixing_blocks):
    first_scale = 1.0 / math.sqrt(C)
    scale_two = 1.0 / math.sqrt(R)
    gated = (inputs.astype(jnp.float32) * gate_in.astype(jnp.float32)).astype(jnp.bfloat16)
    grad_second = (cotangent.astype(jnp.float32) * gate_out.astype(jnp.float32)).astype(jnp.bfloat16)
    incoming_rows = jnp.transpose(gated, (1, 0, 2))

    def forward_row(pair):
        weight, values = pair
        return (jnp.dot(values, weight.T, preferred_element_type=jnp.float32) * first_scale).astype(jnp.bfloat16)
    first_rows = lax.map(forward_row, (mix_one, incoming_rows))
    first_cols = jnp.transpose(first_rows, (2, 1, 0))

    def column_step(triple):
        weight, values, grads = triple
        second = (jnp.dot(values, weight.T, preferred_element_type=jnp.float32) * scale_two).astype(jnp.bfloat16)
        back = (jnp.dot(grads, weight, preferred_element_type=jnp.float32) * scale_two).astype(jnp.bfloat16)
        weight_grad = (jnp.dot(grads.T, values, preferred_element_type=jnp.float32) * scale_two).astype(jnp.bfloat16)
        return (second, back, weight_grad)
    second, back_cols, grad_mix_two = lax.map(column_step, (second_mixing_blocks, first_cols, grad_second))
    grad_gate_out = (cotangent.astype(jnp.float32) * second.astype(jnp.float32)).astype(jnp.bfloat16)
    backward_row_values = jnp.transpose(back_cols, (2, 1, 0))

    def row_step(triple):
        weight, values, grads = triple
        grouped_gradient = grads.reshape(D, N_CHAN, C // N_CHAN).astype(jnp.float32)
        grouped_weight = weight.reshape(N_CHAN, C // N_CHAN, C).astype(jnp.float32)
        summand_terms = (jnp.einsum('kmv,mvj->mkj', grouped_gradient, grouped_weight) * first_scale).astype(jnp.bfloat16)
        back = lax.optimization_barrier(jnp.sum(summand_terms.astype(jnp.float32), axis=0)).astype(jnp.bfloat16)
        weight_grad = (jnp.dot(grads.T, values, preferred_element_type=jnp.float32) * first_scale).astype(jnp.bfloat16)
        return (back, weight_grad)
    back_in_rows, grad_mix_one = lax.map(row_step, (mix_one, incoming_rows, backward_row_values))
    grad_gated = jnp.transpose(back_in_rows, (1, 0, 2))
    grad_input = (grad_gated.astype(jnp.float32) * gate_in.astype(jnp.float32)).astype(jnp.bfloat16)
    return (grad_input, grad_gate_out, grad_mix_one, grad_mix_two)
```

```python
import math

import jax
import jax.numpy as jnp
from jax import lax
from jax.sharding import PartitionSpec as P


CHUNKS = 4


def f32(x):
    return x.astype(jnp.float32)


def bf16(x):
    return x.astype(jnp.bfloat16)


def dot(spec, a, b):
    return jnp.einsum(spec, a, b, preferred_element_type=jnp.float32)


def gather_half(own):
    count = lax.axis_size("chan")
    if count != 2:
        return lax.all_gather(own, "chan", axis=1, tiled=True)
    own, me = lax.optimization_barrier((own, lax.axis_index("chan")))
    first_of_two = me == 0
    other = lax.ppermute(own, "chan", [(0, 1), (1, 0)])
    return jnp.concatenate(
        [jnp.where(first_of_two, own, other), jnp.where(first_of_two, other, own)], axis=1
    )


def reduce_ring(partial_of):
    count = lax.axis_size("chan")
    me = lax.axis_index("chan")
    ring = [(k, (k + 1) % count) for k in range(count)]
    total = None
    for step in range(count):
        block = lax.rem(me + (2 * count - 1 - step), count)
        part = partial_of(block)
        total = part if total is None else part + f32(total)
        if step < count - 1:
            total = bf16(total)
            total = lax.ppermute(total, "chan", ring)
    return bf16(total)


def shards(inputs, gate_in, gate_out, cotangent, mix_one, second_mixing_blocks):
    count = lax.axis_size("chan")
    seq = lax.axis_size("seq")
    one_scale = 1.0 / math.sqrt(mix_one.shape[2])
    two_scale = 1.0 / math.sqrt(second_mixing_blocks.shape[2])
    rows = mix_one.shape[0]
    cols = second_mixing_blocks.shape[0]
    chans = inputs.shape[0]
    chunks = math.gcd(CHUNKS, rows)

    weights_one = [gather_half(w) for w in jnp.split(mix_one, chunks, axis=0)]
    weights_two = [gather_half(w) for w in jnp.split(second_mixing_blocks, chunks, axis=0)]
    gated = bf16(f32(inputs) * f32(gate_in))
    grad_second = bf16(f32(cotangent) * f32(gate_out))

    parts = []
    for w, x in zip(weights_one, jnp.split(gated, chunks, axis=1)):
        first = bf16(dot("roi,dri->odr", w, x) * one_scale)
        first = first.reshape(seq, cols, chans, first.shape[2])
        got = lax.all_to_all(first, "seq", split_axis=0, concat_axis=0)
        parts.append(got)
    first_cols = jnp.stack(parts, axis=0)
    first_cols = jnp.transpose(first_cols, (2, 3, 1, 0, 4)).reshape(cols, chans, seq * rows)

    backs = []
    for w, g in zip(weights_two, jnp.split(grad_second, chunks, axis=0)):
        back = bf16(dot("coi,cdo->icd", w, g) * two_scale)
        back = back.reshape(seq, rows, back.shape[1], chans)
        got = lax.all_to_all(back, "seq", split_axis=0, concat_axis=0)
        backs.append(got)
    grad_first = jnp.stack(backs, axis=0)
    grad_first = jnp.transpose(grad_first, (2, 1, 0, 3, 4)).reshape(rows, seq * cols, chans)

    half_two = grad_second.shape[2] // count
    half_one = (seq * cols) // count

    def part_two(block):
        g = lax.dynamic_slice_in_dim(grad_second, block * half_two, half_two, axis=2)
        return dot("cdo,cdi->coi", g, first_cols) * two_scale

    def part_one(block):
        g = lax.dynamic_slice_in_dim(grad_first, block * half_one, half_one, axis=1)
        return dot("rod,dri->roi", g, gated) * one_scale

    grad_mix_two = reduce_ring(part_two)
    grad_mix_one = reduce_ring(part_one)

    full_two = jnp.concatenate(weights_two, axis=0)
    full_one = jnp.concatenate(weights_one, axis=0)
    second = bf16(dot("coi,cdi->cdo", full_two, first_cols) * two_scale)
    grad_gate_out = bf16(f32(cotangent) * f32(second))
    grad_gated = bf16(dot("roi,rod->dri", full_one, grad_first) * one_scale)
    grad_input = bf16(f32(grad_gated) * f32(gate_in))
    return (grad_input, grad_gate_out, grad_mix_one, grad_mix_two)


def solution(mesh):
    rows_first = P("seq", "chan", None)
    chan_first = P("chan", "seq", None)
    return jax.shard_map(
        shards,
        mesh=mesh,
        in_specs=(chan_first, chan_first, rows_first, rows_first, rows_first, rows_first),
        out_specs=(chan_first, rows_first, rows_first, rows_first),
        check_vma=False,
    )
```
